32 devices in a mesh: scen: 4 (over y, core), row: 8 (over z, x).
Axes of the slice: x: 2, y: 2, z: 4, core: 2. Of those that a mesh axis runs over, the one named last changes fastest.
Arguments:
- borders: bfloat16 [4, 1024, 12288], P('scen', None, 'row'), may hold values from -1.078125 to 1.078125
- kkt_inverse: bfloat16 [4, 1024, 1024], P('scen', 'row'), may hold values from -0.35 to 2.35, as said below
- first_section: float32 [12288, 256], P('row'), may hold values from -6 to 6
- barrier: float32 [12288], P('row'), may hold values from 64 to 512
- panel_vars: int32 [256], replicated, may hold values from 0 to 12287, as said below
- probability: float32 [4], replicated, may hold values from 0.5 to 2
- assignment: int32 [4], P('scen'), may hold values from 0 to 3, each once
Outputs:
- factor: float32 [12288, 256], P('row')
The draws below stay inside these ranges and needn't reach their ends.
Inputs may be any that keep to these rules, and one draw needn't show every extreme that they name: `panel_vars`: distinct values. `kkt_inverse`: each scenario's matrix is symmetric positive definite. `assignment`: each scenario once.
All inputs are finite; a program needn't handle non-finite values.
Results may differ from the reference program's by a relative error of at most 0.00031.
Values may be sent and summed in bfloat16 or wider, within the bound.
A program may use at most 64 MiB of HBM per device.

```python
import math
import jax
import jax.numpy as jnp
from jax import lax

N0 = 12288
NS = 1024
PANEL = 128
PANELS = 2
WIN = 256
SCENARIOS = 4


def draw_panel_vars(key, part):
    chosen = jax.random.permutation(jax.random.fold_in(key, 11), N0)
    return chosen[:WIN].astype(jnp.int32)


def draw_kkt_inverse(key, part):
    noise_key, diag_key = jax.random.split(jax.random.fold_in(key, 23))
    noise = jnp.clip(jax.random.normal(noise_key, (SCENARIOS, NS, NS), jnp.float32), -3.0, 3.0)
    symmetric = (noise + jnp.swapaxes(noise, 1, 2)) * (0.4 / math.sqrt(2.0 * NS))
    diagonal = jnp.exp(jax.random.uniform(diag_key, (SCENARIOS, NS), jnp.float32, 0.0, math.log(2.0)))
    result = symmetric + diagonal[:, :, None] * jnp.eye(NS, dtype=jnp.float32)[None, :, :]
    return result.astype(jnp.bfloat16)


def levels(rng, extent, cuts, smallest, high):
    def one(position, parts):
        draws = jax.random.uniform(jax.random.fold_in(jax.random.fold_in(rng, 6), position), (parts,), jnp.float32, smallest / len(cuts), high / len(cuts))
        return jnp.repeat(jnp.exp(draws), extent[position] // parts).reshape((-1,) + (1,) * (len(extent) - position - 1))

    level = one(*cuts[0])
    for cut in cuts[1:]:
        level = level * one(*cut)
    return level


def normal_values(rng, extent, deviation, reach, pieces=(), kind=jnp.bfloat16):
    loudness = levels(rng, extent, pieces, -0.22, 0.18) if pieces else 1.0
    entries = jax.random.normal(rng, extent, jnp.float32) * deviation * loudness
    return jnp.minimum(jnp.maximum(entries, -reach), reach).astype(kind)


def setup_inputs(seed: int = 0) -> dict:
    streams_of = jax.random.split(jax.random.key(seed), 8)
    return {
        "borders": normal_values(streams_of[0], (SCENARIOS, NS, N0), 0.18, 1.078125, ((0, 4), (2, 8))),
        "kkt_inverse": draw_kkt_inverse(jax.random.fold_in(streams_of[7], 71), 0),
        "first_section": normal_values(streams_of[2], (N0, WIN), 1.0, 6.0, ((0, 8),), jnp.float32),
        "barrier": jnp.clip(jnp.exp(math.log(512.0) - 2.0794415 * jax.random.uniform(streams_of[3], (N0,), jnp.float32) ** levels(streams_of[3], (N0,), ((0, 8),), -0.2, 0.2)), 64.0, 512.0),
        "panel_vars": draw_panel_vars(jax.random.fold_in(streams_of[7], 71), 0),
        "probability": jnp.clip(jnp.exp(jax.random.uniform(streams_of[5], (SCENARIOS,), jnp.float32, math.log(0.5), math.log(2.0))), 0.5, 2.0),
        "assignment": jax.random.permutation(streams_of[6], SCENARIOS).astype(jnp.int32),
    }


def factorize(diag_block, row_block):
    symmetric = 0.5 * (diag_block + diag_block.T)
    block_parts = []
    row_parts = []
    for panel_index in range(PANELS):
        low_col = panel_index * PANEL
        high_col = low_col + PANEL
        block_cols = symmetric[:, low_col:high_col]
        row_cols = row_block[:, low_col:high_col]
        if panel_index > 0:
            earlier_block = jnp.concatenate(block_parts, axis=1)
            earlier_rows = jnp.concatenate(row_parts, axis=1)
            across = earlier_block[low_col:high_col, :]
            block_cols = block_cols - jnp.dot(earlier_block, across.T, precision=lax.Precision.HIGHEST)
            row_cols = row_cols - jnp.dot(earlier_rows, across.T, precision=lax.Precision.HIGHEST)
        panel_chol = jnp.linalg.cholesky(block_cols[low_col:high_col, :])
        block_parts.append(lax.linalg.triangular_solve(panel_chol, block_cols, left_side=False, lower=True, transpose_a=True))
        row_parts.append(lax.linalg.triangular_solve(panel_chol, row_cols, left_side=False, lower=True, transpose_a=True))
    return jnp.concatenate(row_parts, axis=1)

def reference(borders, kkt_inverse, first_section, barrier, panel_vars, probability, assignment):
    scen_count = borders.shape[0]
    picked = jnp.take(borders, panel_vars, axis=2)
    weights = jnp.take(probability, assignment)

    def accumulate(scen_index, total):
        inverse = lax.dynamic_index_in_dim(kkt_inverse, scen_index, 0, keepdims=False)
        columns = lax.dynamic_index_in_dim(picked, scen_index, 0, keepdims=False)
        border = lax.dynamic_index_in_dim(borders, scen_index, 0, keepdims=False)
        solved = jnp.dot(inverse.astype(jnp.float32), columns.astype(jnp.float32), preferred_element_type=jnp.float32).astype(jnp.bfloat16)
        term = lax.dot_general(border.astype(jnp.float32), solved.astype(jnp.float32), (((0,), (0,)), ((), ())), preferred_element_type=jnp.float32)
        return total + weights[scen_index] * term
    total = lax.fori_loop(0, scen_count, accumulate, jnp.zeros((N0, WIN), jnp.float32))
    hits = jnp.arange(N0, dtype=jnp.int32)[:, None] == panel_vars[None, :]
    schur = total + first_section + jnp.where(hits, barrier[:, None], jnp.zeros((), jnp.float32))
    diag_block = jnp.take(schur, panel_vars, axis=0)
    return factorize(diag_block, schur)
```

```python
import functools

import jax
import jax.numpy as jnp
from jax import lax
from jax.experimental import pallas as pl
from jax.experimental.pallas import tpu as pltpu
from jax.sharding import PartitionSpec as P

PANEL = 128
MESH = pl.DeviceIdType.MESH
HIGH = lax.Precision.HIGHEST
F32 = jnp.float32
BF16 = jnp.bfloat16
CHUNKS = 4


def factorize(symmetric, row_block):
    window = symmetric.shape[0]
    block_parts = []
    row_parts = []
    for low_col in range(0, window, PANEL):
        high_col = low_col + PANEL
        block_cols = symmetric[:, low_col:high_col]
        row_cols = row_block[:, low_col:high_col]
        if low_col > 0:
            earlier_block = jnp.concatenate(block_parts, axis=1)
            earlier_rows = jnp.concatenate(row_parts, axis=1)
            across = earlier_block[low_col:high_col, :]
            block_cols = block_cols - jnp.dot(earlier_block, across.T, precision=HIGH)
            row_cols = row_cols - jnp.dot(earlier_rows, across.T, precision=HIGH)
        panel_chol = jnp.linalg.cholesky(block_cols[low_col:high_col, :])
        block_parts.append(
            lax.linalg.triangular_solve(
                panel_chol, block_cols, left_side=False, lower=True, transpose_a=True
            )
        )
        row_parts.append(
            lax.linalg.triangular_solve(
                panel_chol, row_cols, left_side=False, lower=True, transpose_a=True
            )
        )
    return jnp.concatenate(row_parts, axis=1)


def flip(index, bit):
    return index + bit * (1 - 2 * ((index // bit) % 2))


def toggle(index, mask):
    bit = 1
    while bit <= mask:
        if mask & bit:
            index = flip(index, bit)
        bit *= 2
    return index


def bits_down(count):
    bits = []
    bit = count // 2
    while bit >= 1:
        bits.append(bit)
        bit //= 2
    return bits


def low_bit(mask):
    return mask & -mask


def gather_blocks(held, me, count, send_sem, recv_sem):
    bits = bits_down(count)

    def copy(mask, bit):
        owner = toggle(me, mask)
        return pltpu.make_async_remote_copy(
            src_ref=held.at[owner],
            dst_ref=held.at[owner],
            send_sem=send_sem.at[mask + bit],
            recv_sem=recv_sem.at[mask + bit],
            device_id={"row": flip(me, bit)},
            device_id_type=MESH,
        )

    order = [0]
    for bit in bits:
        order += [mask + bit for mask in list(order)]
    sent = []
    for mask in order:
        if mask:
            landed = pltpu.make_async_remote_copy(
                src_ref=held.at[toggle(me, mask)],
                dst_ref=held.at[toggle(me, mask)],
                send_sem=send_sem.at[mask],
                recv_sem=recv_sem.at[mask],
                device_id={"row": flip(me, low_bit(mask))},
                device_id_type=MESH,
            )
            landed.wait_recv()
        for bit in bits:
            if mask == 0 or bit < low_bit(mask):
                one = copy(mask, bit)
                one.start()
                sent.append(one)
    return sent


def schur_kernel(
    n_scen, n_row,
    pv_row, pv_col, prob, asg, b_ref, k_ref, base,
    diag, h_ref,
    onehot, picked, parts, columns, solved, fpick, fparts, fall, bt,
    t_own, t_in, t_sum, out_half, in_half, mine, y_in,
    rs_send, rs_recv, fs_send, fs_recv, agc_send, agc_recv, agf_send, agf_recv,
    ags_send, ags_recv, t_send, t_recv, c_send, c_recv, y_send, y_recv,
    g_send, g_recv,
):
    scen = lax.axis_index("scen")
    row = lax.axis_index("row")
    depth = picked.shape[1]
    rows, window = base.shape
    barrier = pltpu.get_barrier_semaphore()
    scen_bits = bits_down(n_scen)[::-1]
    for step in range(1, n_row):
        pl.semaphore_signal(
            barrier, inc=1, device_id={"row": (row + step) % n_row}, device_id_type=MESH
        )
    for bit in scen_bits:
        pl.semaphore_signal(
            barrier, inc=1, device_id={"scen": flip(scen, bit)}, device_id_type=MESH
        )

    first = row * rows
    local = pv_row[...] - first
    onehot[...] = jnp.where(
        lax.broadcasted_iota(jnp.int32, (rows, window), 0) == local, 1.0, 0.0
    ).astype(BF16)

    fgroups = fpick.shape[0]
    del fgroups
    frows = fpick.shape[0] * fpick.shape[1]
    groups = window // frows
    fstart = pl.multiple_of((scen % groups) * frows, 8)
    flocal = pv_col[pl.ds(fstart, frows), :] - first
    fhot = jnp.where(
        lax.broadcasted_iota(jnp.int32, (frows, rows), 1) == flocal, 1.0, 0.0
    ).astype(F32)

    pl.semaphore_wait(barrier, n_row - 1 + len(scen_bits))

    def pick(dst):
        start = pl.multiple_of(dst * depth, depth)
        block = jnp.dot(
            b_ref[pl.ds(start, depth), :], onehot[...], preferred_element_type=F32
        )
        return block.astype(BF16)

    def rs_copy(src, dst_ref, send, recv, dst, slot_send, slot_recv):
        return pltpu.make_async_remote_copy(
            src_ref=src,
            dst_ref=dst_ref,
            send_sem=send.at[slot_send],
            recv_sem=recv.at[slot_recv],
            device_id={"row": dst},
            device_id_type=MESH,
        )

    def send_pick(step, carry):
        dst = (row + step) % n_row
        picked[dst] = pick(dst)
        rs_copy(picked.at[dst], parts.at[row], rs_send, rs_recv, dst, dst, row).start()
        return carry

    lax.fori_loop(1, n_row, send_pick, 0)
    parts[row] = pick(row)

    fpick[...] = jnp.dot(
        fhot, base[...], preferred_element_type=F32, precision=HIGH
    ).reshape(fpick.shape)
    for step in range(1, n_row):
        dst = (row + step) % n_row
        rs_copy(fpick.at[dst], fparts.at[row], fs_send, fs_recv, dst, dst, row).start()
    fparts[row] = fpick[row]

    def turn(tile, carry):
        start = pl.multiple_of(tile * PANEL, PANEL)
        bt[pl.ds(start, PANEL), :] = b_ref[:, pl.ds(start, PANEL)].T
        return carry

    lax.fori_loop(0, rows // PANEL, turn, 0)

    for step in range(1, n_row):
        src = (row + n_row - step) % n_row
        rs_copy(picked.at[src], parts.at[src], rs_send, rs_recv, src, src, src).wait_recv()
    total = parts[0].astype(F32)
    for slot in range(1, n_row):
        total = total + parts[slot].astype(F32)
    columns[row] = total.astype(BF16)
    sent = gather_blocks(columns, row, n_row, agc_send, agc_recv)

    own = jnp.dot(
        k_ref[...],
        columns[...].reshape(n_row * depth, window),
        preferred_element_type=F32,
    )
    solved[row] = own.astype(BF16)
    sent += gather_blocks(solved, row, n_row, ags_send, ags_recv)

    for step in range(1, n_row):
        src = (row + n_row - step) % n_row
        rs_copy(fpick.at[src], fparts.at[src], fs_send, fs_recv, src, src, src).wait_recv()
    ftotal = fparts[0]
    for slot in range(1, n_row):
        ftotal = ftotal + fparts[slot]
    fall[row] = ftotal
    sent += gather_blocks(fall, row, n_row, agf_send, agf_recv)

    match = lax.broadcasted_iota(jnp.int32, prob.shape, 1) == asg[...]
    weight = jnp.sum(jnp.where(match, prob[...], 0.0), axis=1, keepdims=True)

    t_own[...] = weight * lax.dot_general(
        columns[...].reshape(n_row * depth, window),
        solved[...].reshape(n_row * depth, window),
        (((0,), (0,)), ((), ())),
        preferred_element_type=F32,
    )
    keep = jnp.where(scen < groups, 1.0, 0.0)
    t_own[pl.ds(fstart, frows), :] += fall[...].reshape(frows, window) * keep

    def t_copy(index, bit, src):
        return pltpu.make_async_remote_copy(
            src_ref=src,
            dst_ref=t_in.at[index],
            send_sem=t_send.at[index],
            recv_sem=t_recv.at[index],
            device_id={"scen": flip(scen, bit)},
            device_id_type=MESH,
        )

    def t_src(index):
        return t_own if index == 0 else t_sum.at[index - 1]

    t_copy(0, scen_bits[0], t_own).start()

    half = rows // 2
    chunk = half // CHUNKS
    core = scen % 2

    def term(which, part):
        start = pl.multiple_of(which * half + part * chunk, 8)
        return weight * jnp.dot(
            bt[pl.ds(start, chunk), :],
            solved[...].reshape(n_row * depth, window),
            preferred_element_type=F32,
        )

    def c_copy(part):
        return pltpu.make_async_remote_copy(
            src_ref=out_half.at[part],
            dst_ref=in_half.at[part],
            send_sem=c_send.at[part],
            recv_sem=c_recv.at[part],
            device_id={"scen": flip(scen, 1)},
            device_id_type=MESH,
        )

    def y_copy(index, bit, part):
        return pltpu.make_async_remote_copy(
            src_ref=mine.at[index, part],
            dst_ref=y_in.at[index, part],
            send_sem=y_send.at[index, part],
            recv_sem=y_recv.at[index, part],
            device_id={"scen": flip(scen, bit)},
            device_id_type=MESH,
        )

    for part in range(CHUNKS):
        out_half[part] = term(1 - core, part)
        c_copy(part).start()

    def t_step(index):
        copy = t_copy(index, scen_bits[index], t_src(index))
        copy.wait_recv()
        t_sum[index] = t_src(index)[...] + t_in[index]
        if index + 1 < len(scen_bits):
            t_copy(index + 1, scen_bits[index + 1], t_sum.at[index]).start()

    for part in range(CHUNKS):
        mine[0, part] = term(core, part)
    t_step(0)
    y_bits = scen_bits[1:]
    for part in range(CHUNKS):
        c_copy(part).wait_recv()
        mine[0, part] += in_half[part]
        y_copy(0, y_bits[0], part).start()
    for index in range(1, len(scen_bits)):
        t_step(index)
    whole = t_sum[len(scen_bits) - 1]
    diag[...] = 0.5 * (whole + whole.T)

    def g_copy(part):
        start = pl.multiple_of(core * half + part * chunk, 8)
        return pltpu.make_async_remote_copy(
            src_ref=mine.at[len(y_bits), part],
            dst_ref=h_ref.at[pl.ds(start, chunk), :],
            send_sem=g_send.at[part],
            recv_sem=g_recv.at[part],
            device_id={"scen": flip(scen, 1)},
            device_id_type=MESH,
        )

    for index, bit in enumerate(y_bits):
        for part in range(CHUNKS):
            y_copy(index, bit, part).wait_recv()
            total_part = mine[index, part] + y_in[index, part]
            start = pl.multiple_of(core * half + part * chunk, 8)
            if index + 1 == len(y_bits):
                total_part = total_part + base[pl.ds(start, chunk), :]
            mine[index + 1, part] = total_part
            if index + 1 < len(y_bits):
                y_copy(index + 1, y_bits[index + 1], part).start()
            else:
                h_ref[pl.ds(start, chunk), :] = total_part
                g_copy(part).start()
    for part in range(CHUNKS):
        g_copy(part).wait()

    for one in sent:
        one.wait_send()
    for step in range(1, n_row):
        dst = (row + step) % n_row
        rs_copy(picked.at[dst], parts.at[row], rs_send, rs_recv, dst, dst, row).wait_send()
        rs_copy(fpick.at[dst], fparts.at[row], fs_send, fs_recv, dst, dst, row).wait_send()
    for index, bit in enumerate(scen_bits):
        t_copy(index, bit, t_src(index)).wait_send()
    for part in range(CHUNKS):
        c_copy(part).wait_send()
        for index, bit in enumerate(y_bits):
            y_copy(index, bit, part).wait_send()


def per_device(
    n_scen, n_row,
    borders, kkt_inverse, first_section, barrier, panel_vars, probability, assignment,
):
    rows, window = first_section.shape
    depth = kkt_inverse.shape[1]
    full = kkt_inverse.shape[2]
    first_row = lax.axis_index("row") * rows
    hits = jnp.arange(rows, dtype=jnp.int32)[:, None] + first_row == panel_vars[None, :]
    base = first_section + jnp.where(hits, barrier[:, None], 0.0)
    groups = max(1, min(n_scen, window // (8 * n_row)))
    frow = window // groups // n_row
    stages = n_scen.bit_length() - 1
    half_chunk = rows // 2 // CHUNKS
    dma = pltpu.SemaphoreType.DMA
    vmem = pl.BlockSpec(memory_space=pltpu.VMEM)
    diag, schur = pl.pallas_call(
        functools.partial(schur_kernel, n_scen, n_row),
        out_shape=(
            jax.ShapeDtypeStruct((window, window), F32),
            jax.ShapeDtypeStruct((rows, window), F32),
        ),
        in_specs=[vmem] * 7,
        out_specs=(vmem, vmem),
        scratch_shapes=[
            pltpu.VMEM((rows, window), BF16),
            pltpu.VMEM((n_row, depth, window), BF16),
            pltpu.VMEM((n_row, depth, window), BF16),
            pltpu.VMEM((n_row, depth, window), BF16),
            pltpu.VMEM((n_row, depth, window), BF16),
            pltpu.VMEM((n_row, frow, window), F32),
            pltpu.VMEM((n_row, frow, window), F32),
            pltpu.VMEM((n_row, frow, window), F32),
            pltpu.VMEM((rows, full), BF16),
            pltpu.VMEM((window, window), F32),
            pltpu.VMEM((stages, window, window), F32),
            pltpu.VMEM((stages, window, window), F32),
            pltpu.VMEM((CHUNKS, half_chunk, window), F32),
            pltpu.VMEM((CHUNKS, half_chunk, window), F32),
            pltpu.VMEM((stages, CHUNKS, half_chunk, window), F32),
            pltpu.VMEM((stages - 1, CHUNKS, half_chunk, window), F32),
            *[dma((n_row,))] * 10,
            dma((stages,)), dma((stages,)),
            dma((CHUNKS,)), dma((CHUNKS,)),
            dma((stages - 1, CHUNKS)), dma((stages - 1, CHUNKS)),
            dma((CHUNKS,)), dma((CHUNKS,)),
        ],
        compiler_params=pltpu.CompilerParams(collective_id=0, has_side_effects=True),
    )(
        panel_vars[None, :], panel_vars[:, None], probability[None, :],
        assignment[:, None], borders[0], kkt_inverse[0], base,
    )
    return factorize(diag, schur)


def solution(mesh):
    placed = (
        P("scen", None, "row"),
        P("scen", "row", None),
        P("row", None),
        P("row"),
        P(),
        P(),
        P("scen"),
    )
    return jax.shard_map(
        functools.partial(per_device, mesh.shape["scen"], mesh.shape["row"]),
        mesh=mesh, in_specs=placed, out_specs=P("row", None), check_vma=False,
    )
```

```python
import functools

import jax
import jax.numpy as jnp
from jax import lax
from jax.experimental import pallas as pl
from jax.experimental.pallas import tpu as pltpu
from jax.sharding import PartitionSpec as P

PANEL = 128
MESH = pl.DeviceIdType.MESH
HIGH = lax.Precision.HIGHEST
F32 = jnp.float32
BF16 = jnp.bfloat16
CHUNKS = 4
SUB = 8
BLOCK = 64


def panel_inverse(block, size):
    panel = block.shape[0]
    sub = lax.broadcasted_iota(jnp.int32, (SUB, panel), 0)
    lane = lax.broadcasted_iota(jnp.int32, (SUB, panel), 1)
    left = [block[low:low + SUB, :] for low in range(0, panel, SUB)]
    right = [
        jnp.where(lane == sub + low, 1.0, 0.0) for low in range(0, panel, SUB)
    ]
    per = size // SUB
    for base in range(0, panel // SUB, per):
        for col in range(base * SUB, (base + per) * SUB):
            own, line = col // SUB, col % SUB
            scale = lax.rsqrt(left[own][line:line + 1, col:col + 1])
            row_left = left[own][line:line + 1, :] * scale
            row_right = right[own][line:line + 1, :] * scale
            for tile in range(own, base + per):
                factor = left[tile][:, col:col + 1] * scale
                next_left = left[tile] - factor * row_left
                next_right = right[tile] - factor * row_right
                if tile == own:
                    next_left = jnp.where(sub > line, next_left, left[tile])
                    next_right = jnp.where(sub > line, next_right, right[tile])
                    next_left = jnp.where(sub == line, row_left, next_left)
                    next_right = jnp.where(sub == line, row_right, next_right)
                left[tile], right[tile] = next_left, next_right
        if base + per < panel // SUB:
            upper = jnp.concatenate(left[base:base + per], axis=0)
            both = jnp.concatenate(
                [upper, jnp.concatenate(right[base:base + per], axis=0)], axis=1
            )
            change = lax.dot_general(
                upper, both, (((0,), (0,)), ((), ())),
                precision=HIGH, preferred_element_type=F32,
            )
            for tile in range(base + per, panel // SUB):
                low = tile * SUB
                left[tile] = left[tile] - change[low:low + SUB, :panel]
                right[tile] = right[tile] - change[low:low + SUB, panel:]
    return jnp.concatenate(right, axis=0)


def flip(index, bit):
    return index + bit * (1 - 2 * ((index // bit) % 2))


def toggle(index, mask):
    bit = 1
    while bit <= mask:
        if mask & bit:
            index = flip(index, bit)
        bit *= 2
    return index


def bits_down(count):
    bits = []
    bit = count // 2
    while bit >= 1:
        bits.append(bit)
        bit //= 2
    return bits


def low_bit(mask):
    return mask & -mask


def gather_blocks(held, me, count, send_sem, recv_sem):
    bits = bits_down(count)

    def copy(mask, bit):
        owner = toggle(me, mask)
        return pltpu.make_async_remote_copy(
            src_ref=held.at[owner],
            dst_ref=held.at[owner],
            send_sem=send_sem.at[mask + bit],
            recv_sem=recv_sem.at[mask + bit],
            device_id={"row": flip(me, bit)},
            device_id_type=MESH,
        )

    order = [0]
    for bit in bits:
        order += [mask + bit for mask in list(order)]
    sent = []
    for mask in order:
        if mask:
            landed = pltpu.make_async_remote_copy(
                src_ref=held.at[toggle(me, mask)],
                dst_ref=held.at[toggle(me, mask)],
                send_sem=send_sem.at[mask],
                recv_sem=recv_sem.at[mask],
                device_id={"row": flip(me, low_bit(mask))},
                device_id_type=MESH,
            )
            landed.wait_recv()
        for bit in bits:
            if mask == 0 or bit < low_bit(mask):
                one = copy(mask, bit)
                one.start()
                sent.append(one)
    return sent


def schur_kernel(
    n_scen, n_row,
    pv_row, prob, asg, bar_row, b_ref, k_ref, base,
    f_ref,
    h_ref, pv_col, onehot, picked, parts, columns, solved, fpick, fparts, fall, bt,
    t_own, t_in, t_sum, out_half, in_half, mine, y_in,
    rs_send, rs_recv, fs_send, fs_recv, agc_send, agc_recv, agf_send, agf_recv,
    ags_send, ags_recv, t_send, t_recv, c_send, c_recv, y_send, y_recv,
    g_send, g_recv,
):
    scen = lax.axis_index("scen")
    row = lax.axis_index("row")
    depth = picked.shape[1]
    rows, window = base.shape
    barrier = pltpu.get_barrier_semaphore()
    scen_bits = bits_down(n_scen)[::-1]
    for step in range(1, n_row):
        pl.semaphore_signal(
            barrier, inc=1, device_id={"row": (row + step) % n_row}, device_id_type=MESH
        )
    for bit in scen_bits:
        pl.semaphore_signal(
            barrier, inc=1, device_id={"scen": flip(scen, bit)}, device_id_type=MESH
        )

    first = row * rows
    local = pv_row[...] - first
    onehot[...] = jnp.where(
        lax.broadcasted_iota(jnp.int32, (rows, window), 0) == local, 1.0, 0.0
    ).astype(BF16)

    frows = fpick.shape[0] * fpick.shape[1]
    groups = window // frows
    fstart = pl.multiple_of((scen % groups) * frows, 8)
    pv_col[...] = jnp.broadcast_to(pv_row[...], (SUB, window)).T
    flocal = pv_col[pl.ds(fstart, frows), 0:1] - first
    fhot = jnp.where(
        lax.broadcasted_iota(jnp.int32, (frows, rows), 1) == flocal, 1.0, 0.0
    ).astype(F32)

    pl.semaphore_wait(barrier, n_row - 1 + len(scen_bits))

    def pick(dst):
        start = pl.multiple_of(dst * depth, depth)
        block = jnp.dot(
            b_ref[pl.ds(start, depth), :], onehot[...], preferred_element_type=F32
        )
        return block.astype(BF16)

    def rs_copy(src, dst_ref, send, recv, dst, slot_send, slot_recv):
        return pltpu.make_async_remote_copy(
            src_ref=src,
            dst_ref=dst_ref,
            send_sem=send.at[slot_send],
            recv_sem=recv.at[slot_recv],
            device_id={"row": dst},
            device_id_type=MESH,
        )

    def send_pick(step, carry):
        dst = (row + step) % n_row
        picked[dst] = pick(dst)
        rs_copy(picked.at[dst], parts.at[row], rs_send, rs_recv, dst, dst, row).start()
        return carry

    lax.fori_loop(1, n_row, send_pick, 0)
    parts[row] = pick(row)

    bsel = jnp.dot(
        jnp.broadcast_to(bar_row[...], (SUB, rows)), onehot[...].astype(F32),
        preferred_element_type=F32, precision=HIGH,
    )[0:1, :]
    slot_row = lax.broadcasted_iota(jnp.int32, (frows, window), 0) + fstart
    slot_col = lax.broadcasted_iota(jnp.int32, (frows, window), 1)
    fpick[...] = (
        jnp.dot(fhot, base[...], preferred_element_type=F32, precision=HIGH)
        + jnp.where(slot_row == slot_col, bsel, 0.0)
    ).reshape(fpick.shape)
    for step in range(1, n_row):
        dst = (row + step) % n_row
        rs_copy(fpick.at[dst], fparts.at[row], fs_send, fs_recv, dst, dst, row).start()
    fparts[row] = fpick[row]

    def turn(tile, carry):
        start = pl.multiple_of(tile * PANEL, PANEL)
        bt[pl.ds(start, PANEL), :] = b_ref[:, pl.ds(start, PANEL)].T
        return carry

    lax.fori_loop(0, rows // PANEL, turn, 0)

    for step in range(1, n_row):
        src = (row + n_row - step) % n_row
        rs_copy(picked.at[src], parts.at[src], rs_send, rs_recv, src, src, src).wait_recv()
    total = parts[0].astype(F32)
    for slot in range(1, n_row):
        total = total + parts[slot].astype(F32)
    columns[row] = total.astype(BF16)
    sent = gather_blocks(columns, row, n_row, agc_send, agc_recv)

    own = jnp.dot(
        k_ref[...],
        columns[...].reshape(n_row * depth, window),
        preferred_element_type=F32,
    )
    solved[row] = own.astype(BF16)
    sent += gather_blocks(solved, row, n_row, ags_send, ags_recv)

    for step in range(1, n_row):
        src = (row + n_row - step) % n_row
        rs_copy(fpick.at[src], fparts.at[src], fs_send, fs_recv, src, src, src).wait_recv()
    ftotal = fparts[0]
    for slot in range(1, n_row):
        ftotal = ftotal + fparts[slot]
    fall[row] = ftotal
    sent += gather_blocks(fall, row, n_row, agf_send, agf_recv)

    match = lax.broadcasted_iota(jnp.int32, prob.shape, 1) == asg[...]
    weight = jnp.sum(jnp.where(match, prob[...], 0.0), axis=1, keepdims=True)

    t_own[...] = weight * lax.dot_general(
        columns[...].reshape(n_row * depth, window),
        solved[...].reshape(n_row * depth, window),
        (((0,), (0,)), ((), ())),
        preferred_element_type=F32,
    )
    keep = jnp.where(scen < groups, 1.0, 0.0)
    t_own[pl.ds(fstart, frows), :] += fall[...].reshape(frows, window) * keep

    def t_copy(index, bit, src):
        return pltpu.make_async_remote_copy(
            src_ref=src,
            dst_ref=t_in.at[index],
            send_sem=t_send.at[index],
            recv_sem=t_recv.at[index],
            device_id={"scen": flip(scen, bit)},
            device_id_type=MESH,
        )

    def t_src(index):
        return t_own if index == 0 else t_sum.at[index - 1]

    t_copy(0, scen_bits[0], t_own).start()

    half = rows // 2
    chunk = half // CHUNKS
    core = scen % 2

    def term(which, part):
        start = pl.multiple_of(which * half + part * chunk, 8)
        return weight * jnp.dot(
            bt[pl.ds(start, chunk), :],
            solved[...].reshape(n_row * depth, window),
            preferred_element_type=F32,
        )

    def c_copy(part):
        return pltpu.make_async_remote_copy(
            src_ref=out_half.at[part],
            dst_ref=in_half.at[part],
            send_sem=c_send.at[part],
            recv_sem=c_recv.at[part],
            device_id={"scen": flip(scen, 1)},
            device_id_type=MESH,
        )

    def y_copy(index, bit, part):
        return pltpu.make_async_remote_copy(
            src_ref=mine.at[index, part],
            dst_ref=y_in.at[index, part],
            send_sem=y_send.at[index, part],
            recv_sem=y_recv.at[index, part],
            device_id={"scen": flip(scen, bit)},
            device_id_type=MESH,
        )

    for part in range(CHUNKS):
        out_half[part] = term(1 - core, part)
        c_copy(part).start()

    def t_step(index):
        copy = t_copy(index, scen_bits[index], t_src(index))
        copy.wait_recv()
        t_sum[index] = t_src(index)[...] + t_in[index]
        if index + 1 < len(scen_bits):
            t_copy(index + 1, scen_bits[index + 1], t_sum.at[index]).start()

    for part in range(CHUNKS):
        mine[0, part] = term(core, part)
    t_step(0)
    y_bits = scen_bits[1:]
    for part in range(CHUNKS):
        c_copy(part).wait_recv()
        mine[0, part] += in_half[part]
        y_copy(0, y_bits[0], part).start()
    for index in range(1, len(scen_bits)):
        t_step(index)
    whole = t_sum[len(scen_bits) - 1]
    symmetric = 0.5 * (whole + whole.T)
    panels = window // PANEL
    inverses, lowers = [], []

    def matmul_t(lhs, rhs):
        return lax.dot_general(
            lhs, rhs, (((1,), (1,)), ((), ())),
            precision=HIGH, preferred_element_type=F32,
        )

    def next_panel(index):
        low = index * PANEL
        block = symmetric[low:, low:low + PANEL]
        for earlier in range(index):
            rest = lowers[earlier][low - earlier * PANEL:, :]
            block = block - matmul_t(rest, rest[:PANEL, :])
        inverse = panel_inverse(block[:PANEL, :], BLOCK)
        inverses.append(inverse)
        lowers.append(matmul_t(block, inverse))

    next_panel(0)

    def g_copy(part):
        start = pl.multiple_of(core * half + part * chunk, 8)
        return pltpu.make_async_remote_copy(
            src_ref=mine.at[len(y_bits), part],
            dst_ref=h_ref.at[pl.ds(start, chunk), :],
            send_sem=g_send.at[part],
            recv_sem=g_recv.at[part],
            device_id={"scen": flip(scen, 1)},
            device_id_type=MESH,
        )

    for index, bit in enumerate(y_bits):
        for part in range(CHUNKS):
            y_copy(index, bit, part).wait_recv()
            total_part = mine[index, part] + y_in[index, part]
            start = pl.multiple_of(core * half + part * chunk, 8)
            if index + 1 == len(y_bits):
                total_part = total_part + (
                    base[pl.ds(start, chunk), :]
                    + onehot[pl.ds(start, chunk), :].astype(F32) * bsel
                )
            mine[index + 1, part] = total_part
            if index + 1 < len(y_bits):
                y_copy(index + 1, y_bits[index + 1], part).start()
            else:
                h_ref[pl.ds(start, chunk), :] = total_part
                g_copy(part).start()
    for index in range(1, panels):
        next_panel(index)

    def finish(which, part):
        start = pl.multiple_of(which * half + part * chunk, 8)
        done = []
        for index in range(panels):
            low = index * PANEL
            cols = h_ref[pl.ds(start, chunk), low:low + PANEL]
            for earlier in range(index):
                across = lowers[earlier][low - earlier * PANEL:, :][:PANEL, :]
                cols = cols - matmul_t(done[earlier], across)
            done.append(matmul_t(cols, inverses[index]))
            f_ref[pl.ds(start, chunk), low:low + PANEL] = done[index]

    for part in range(CHUNKS):
        finish(core, part)
    for part in range(CHUNKS):
        g_copy(part).wait()
        finish(1 - core, part)

    for one in sent:
        one.wait_send()
    for step in range(1, n_row):
        dst = (row + step) % n_row
        rs_copy(picked.at[dst], parts.at[row], rs_send, rs_recv, dst, dst, row).wait_send()
        rs_copy(fpick.at[dst], fparts.at[row], fs_send, fs_recv, dst, dst, row).wait_send()
    for index, bit in enumerate(scen_bits):
        t_copy(index, bit, t_src(index)).wait_send()
    for part in range(CHUNKS):
        c_copy(part).wait_send()
        for index, bit in enumerate(y_bits):
            y_copy(index, bit, part).wait_send()


def per_device(
    n_scen, n_row,
    borders, kkt_inverse, first_section, barrier, panel_vars, probability, assignment,
):
    rows, window = first_section.shape
    depth = kkt_inverse.shape[1]
    full = kkt_inverse.shape[2]
    groups = max(1, min(n_scen, window // (8 * n_row)))
    frow = window // groups // n_row
    stages = n_scen.bit_length() - 1
    half_chunk = rows // 2 // CHUNKS
    dma = pltpu.SemaphoreType.DMA
    vmem = pl.BlockSpec(memory_space=pltpu.VMEM)
    return pl.pallas_call(
        functools.partial(schur_kernel, n_scen, n_row),
        out_shape=jax.ShapeDtypeStruct((rows, window), F32),
        in_specs=[vmem] * 7,
        out_specs=vmem,
        scratch_shapes=[
            pltpu.VMEM((rows, window), F32),
            pltpu.VMEM((window, SUB), jnp.int32),
            pltpu.VMEM((rows, window), BF16),
            pltpu.VMEM((n_row, depth, window), BF16),
            pltpu.VMEM((n_row, depth, window), BF16),
            pltpu.VMEM((n_row, depth, window), BF16),
            pltpu.VMEM((n_row, depth, window), BF16),
            pltpu.VMEM((n_row, frow, window), F32),
            pltpu.VMEM((n_row, frow, window), F32),
            pltpu.VMEM((n_row, frow, window), F32),
            pltpu.VMEM((rows, full), BF16),
            pltpu.VMEM((window, window), F32),
            pltpu.VMEM((stages, window, window), F32),
            pltpu.VMEM((stages, window, window), F32),
            pltpu.VMEM((CHUNKS, half_chunk, window), F32),
            pltpu.VMEM((CHUNKS, half_chunk, window), F32),
            pltpu.VMEM((stages, CHUNKS, half_chunk, window), F32),
            pltpu.VMEM((stages - 1, CHUNKS, half_chunk, window), F32),
            *[dma((n_row,))] * 10,
            dma((stages,)), dma((stages,)),
            dma((CHUNKS,)), dma((CHUNKS,)),
            dma((stages - 1, CHUNKS)), dma((stages - 1, CHUNKS)),
            dma((CHUNKS,)), dma((CHUNKS,)),
        ],
        compiler_params=pltpu.CompilerParams(collective_id=0, has_side_effects=True),
    )(
        panel_vars[None, :], probability[None, :], assignment[:, None],
        barrier[None, :], borders[0], kkt_inverse[0], first_section,
    )


def solution(mesh):
    placed = (
        P("scen", None, "row"),
        P("scen", "row", None),
        P("row", None),
        P("row"),
        P(),
        P(),
        P("scen"),
    )
    return jax.shard_map(
        functools.partial(per_device, mesh.shape["scen"], mesh.shape["row"]),
        mesh=mesh, in_specs=placed, out_specs=P("row", None), check_vma=False,
    )
```

```python
import functools

import jax
import jax.numpy as jnp
from jax import lax
from jax.experimental import pallas as pl
from jax.experimental.pallas import tpu as pltpu
from jax.sharding import PartitionSpec as P

PANEL = 128
MESH = pl.DeviceIdType.MESH
HIGH = lax.Precision.HIGHEST
F32 = jnp.float32
BF16 = jnp.bfloat16
CHUNKS = 4
SUB = 8
BLOCK = 32


def small_factor(tile, first):
    shape = tile.shape
    spread = [
        jnp.broadcast_to(tile[:, first + k:first + k + 1], shape) for k in range(SUB)
    ]
    cell = {
        (i, k): jnp.broadcast_to(spread[k][i:i + 1, :], shape)
        for k in range(SUB) for i in range(k, SUB)
    }
    scale, lower = [], {}
    for j in range(SUB):
        scale.append(lax.rsqrt(cell[j, j]))
        for i in range(j + 1, SUB):
            lower[i, j] = cell[i, j] * scale[j]
        for k in range(j + 1, SUB):
            for i in range(k, SUB):
                cell[i, k] = cell[i, k] - lower[i, j] * lower[k, j]
    inverse = {}
    for j in range(SUB):
        inverse[j, j] = scale[j]
        for i in range(j + 1, SUB):
            total = lower[i, j] * inverse[j, j]
            for m in range(j + 1, i):
                total = total + lower[i, m] * inverse[m, j]
            inverse[i, j] = -(scale[i] * total)
    return inverse


def panel_inverse(block, size):
    panel = block.shape[0]
    shape = (SUB, panel)
    sub = lax.broadcasted_iota(jnp.int32, shape, 0)
    lane = lax.broadcasted_iota(jnp.int32, shape, 1)
    tiles = panel // SUB
    left = [block[low:low + SUB, :] for low in range(0, panel, SUB)]
    right = [jnp.where(lane == sub + low, 1.0, 0.0) for low in range(0, panel, SUB)]
    per = size // SUB
    for base in range(0, tiles, per):
        for own in range(base, base + per):
            first = own * SUB
            inverse = small_factor(left[own], first)
            new_left = new_right = None
            for k in range(SUB):
                coeff = inverse[SUB - 1, k]
                for i in range(SUB - 2, k - 1, -1):
                    coeff = jnp.where(sub <= i, inverse[i, k], coeff)
                if k:
                    coeff = jnp.where(sub < k, 0.0, coeff)
                add_left = coeff * left[own][k:k + 1, :]
                add_right = coeff * right[own][k:k + 1, :]
                new_left = add_left if k == 0 else new_left + add_left
                new_right = add_right if k == 0 else new_right + add_right
            for tile in range(own + 1, base + per):
                spread = [
                    jnp.broadcast_to(left[tile][:, first + m:first + m + 1], shape)
                    for m in range(SUB)
                ]
                for k in range(SUB):
                    factor = spread[0] * inverse[k, 0]
                    for m in range(1, k + 1):
                        factor = factor + spread[m] * inverse[k, m]
                    left[tile] = left[tile] - factor * new_left[k:k + 1, :]
                    right[tile] = right[tile] - factor * new_right[k:k + 1, :]
            left[own], right[own] = new_left, new_right
        if base + per < tiles:
            upper = jnp.concatenate(left[base:base + per], axis=0)
            both = jnp.concatenate(
                [upper, jnp.concatenate(right[base:base + per], axis=0)], axis=1
            )
            change = lax.dot_general(
                upper, both, (((0,), (0,)), ((), ())),
                precision=HIGH, preferred_element_type=F32,
            )
            for tile in range(base + per, tiles):
                low = tile * SUB
                left[tile] = left[tile] - change[low:low + SUB, :panel]
                right[tile] = right[tile] - change[low:low + SUB, panel:]
    return jnp.concatenate(right, axis=0)


def flip(index, bit):
    return index + bit * (1 - 2 * ((index // bit) % 2))


def toggle(index, mask):
    bit = 1
    while bit <= mask:
        if mask & bit:
            index = flip(index, bit)
        bit *= 2
    return index


def bits_down(count):
    bits = []
    bit = count // 2
    while bit >= 1:
        bits.append(bit)
        bit //= 2
    return bits


def low_bit(mask):
    return mask & -mask


def gather_blocks(arrays, me, count):
    bits = bits_down(count)

    def copy(array, owner, mask, bit):
        held, send_sem, recv_sem = array
        return pltpu.make_async_remote_copy(
            src_ref=held.at[owner],
            dst_ref=held.at[owner],
            send_sem=send_sem.at[mask],
            recv_sem=recv_sem.at[mask],
            device_id={"row": flip(me, bit)},
            device_id_type=MESH,
        )

    order = [0]
    for bit in bits:
        order += [mask + bit for mask in list(order)]
    sent = []
    for mask in order:
        for array in arrays:
            owner = toggle(me, mask)
            if mask:
                copy(array, owner, mask, low_bit(mask)).wait_recv()
            for bit in bits:
                if mask == 0 or bit < low_bit(mask):
                    one = copy(array, owner, mask + bit, bit)
                    one.start()
                    sent.append(one)
    return sent


def schur_kernel(
    n_scen, n_row,
    pv_row, prob, asg, bar_row, b_ref, k_ref, base,
    h_ref, m_ref,
    pv_col, onehot, picked, parts, columns, solved, fpick, fparts, fall, bt,
    t_own, t_in, t_sum, t_all, out_half, in_half, mine, y_in,
    rs_send, rs_recv, fs_send, fs_recv, agc_send, agc_recv, agf_send, agf_recv,
    ags_send, ags_recv, t_send, t_recv, c_send, c_recv, y_send, y_recv,
    g_send, g_recv,
):
    scen = lax.axis_index("scen")
    row = lax.axis_index("row")
    depth = picked.shape[1]
    rows, window = base.shape
    barrier = pltpu.get_barrier_semaphore()
    scen_bits = bits_down(n_scen)[::-1]
    for step in range(1, n_row):
        pl.semaphore_signal(
            barrier, inc=1, device_id={"row": (row + step) % n_row}, device_id_type=MESH
        )
    for bit in scen_bits:
        pl.semaphore_signal(
            barrier, inc=1, device_id={"scen": flip(scen, bit)}, device_id_type=MESH
        )

    first = row * rows
    local = pv_row[...] - first
    onehot[...] = jnp.where(
        lax.broadcasted_iota(jnp.int32, (rows, window), 0) == local, 1.0, 0.0
    ).astype(BF16)

    frows = fpick.shape[0] * fpick.shape[1]
    groups = window // frows
    fstart = pl.multiple_of((scen % groups) * frows, 8)
    pv_col[...] = jnp.broadcast_to(pv_row[...], (SUB, window)).T
    flocal = pv_col[pl.ds(fstart, frows), 0:1] - first
    fhot = jnp.where(
        lax.broadcasted_iota(jnp.int32, (frows, rows), 1) == flocal, 1.0, 0.0
    ).astype(F32)

    pl.semaphore_wait(barrier, n_row - 1 + len(scen_bits))

    def pick(dst):
        start = pl.multiple_of(dst * depth, depth)
        block = jnp.dot(
            b_ref[pl.ds(start, depth), :], onehot[...], preferred_element_type=F32
        )
        return block.astype(BF16)

    def rs_copy(src, dst_ref, send, recv, dst, slot_send, slot_recv):
        return pltpu.make_async_remote_copy(
            src_ref=src,
            dst_ref=dst_ref,
            send_sem=send.at[slot_send],
            recv_sem=recv.at[slot_recv],
            device_id={"row": dst},
            device_id_type=MESH,
        )

    def send_pick(step, carry):
        dst = (row + step) % n_row
        picked[dst] = pick(dst)
        rs_copy(picked.at[dst], parts.at[row], rs_send, rs_recv, dst, dst, row).start()
        return carry

    lax.fori_loop(1, n_row, send_pick, 0)
    parts[row] = pick(row)

    bsel = jnp.dot(
        jnp.broadcast_to(bar_row[...].reshape(1, rows), (SUB, rows)), onehot[...].astype(F32),
        preferred_element_type=F32, precision=HIGH,
    )[0:1, :]
    slot_row = lax.broadcasted_iota(jnp.int32, (frows, window), 0) + fstart
    slot_col = lax.broadcasted_iota(jnp.int32, (frows, window), 1)
    fpick[...] = (
        jnp.dot(fhot, base[...], preferred_element_type=F32, precision=HIGH)
        + jnp.where(slot_row == slot_col, bsel, 0.0)
    ).reshape(fpick.shape)
    for step in range(1, n_row):
        dst = (row + step) % n_row
        rs_copy(fpick.at[dst], fparts.at[row], fs_send, fs_recv, dst, dst, row).start()
    fparts[row] = fpick[row]

    def turn(tile, carry):
        start = pl.multiple_of(tile * PANEL, PANEL)
        bt[pl.ds(start, PANEL), :] = b_ref[:, pl.ds(start, PANEL)].T
        return carry

    lax.fori_loop(0, rows // PANEL, turn, 0)

    for step in range(1, n_row):
        src = (row + n_row - step) % n_row
        rs_copy(picked.at[src], parts.at[src], rs_send, rs_recv, src, src, src).wait_recv()
    total = parts[0].astype(F32)
    for slot in range(1, n_row):
        total = total + parts[slot].astype(F32)
    columns[row] = total.astype(BF16)
    for step in range(1, n_row):
        src = (row + n_row - step) % n_row
        rs_copy(fpick.at[src], fparts.at[src], fs_send, fs_recv, src, src, src).wait_recv()
    ftotal = fparts[0]
    for slot in range(1, n_row):
        ftotal = ftotal + fparts[slot]
    fall[row] = ftotal
    sent = gather_blocks(
        [(columns, agc_send, agc_recv), (fall, agf_send, agf_recv)], row, n_row
    )

    own = jnp.dot(
        k_ref[...],
        columns[...].reshape(n_row * depth, window),
        preferred_element_type=F32,
    )
    solved[row] = own.astype(BF16)
    sent += gather_blocks([(solved, ags_send, ags_recv)], row, n_row)


    match = lax.broadcasted_iota(jnp.int32, prob.shape, 1) == asg[...]
    weight = jnp.sum(jnp.where(match, prob[...], 0.0), axis=1, keepdims=True)

    t_own[...] = weight * lax.dot_general(
        columns[...].reshape(n_row * depth, window),
        solved[...].reshape(n_row * depth, window),
        (((0,), (0,)), ((), ())),
        preferred_element_type=F32,
    )
    keep = jnp.where(scen < groups, 1.0, 0.0)
    t_own[pl.ds(fstart, frows), :] += fall[...].reshape(frows, window) * keep

    core = scen % 2
    t_half = window // 2
    t_mine = pl.multiple_of(core * t_half, 8)
    t_other = pl.multiple_of((1 - core) * t_half, 8)

    def t_copy(index):
        if index == 0:
            src, dst = t_own.at[pl.ds(t_other, t_half), :], t_in.at[0]
        elif index < len(scen_bits):
            src, dst = t_sum.at[index - 1], t_in.at[index]
        else:
            src = t_sum.at[index - 1]
            dst = t_all.at[pl.ds(t_mine, t_half), :]
        return pltpu.make_async_remote_copy(
            src_ref=src,
            dst_ref=dst,
            send_sem=t_send.at[index],
            recv_sem=t_recv.at[index],
            device_id={"scen": flip(scen, (scen_bits + [1])[index])},
            device_id_type=MESH,
        )

    t_copy(0).start()

    half = rows // 2
    chunk = half // CHUNKS
    def term(which, part):
        start = pl.multiple_of(which * half + part * chunk, 8)
        return weight * jnp.dot(
            bt[pl.ds(start, chunk), :],
            solved[...].reshape(n_row * depth, window),
            preferred_element_type=F32,
        )

    def c_copy(part):
        return pltpu.make_async_remote_copy(
            src_ref=out_half.at[part],
            dst_ref=in_half.at[part],
            send_sem=c_send.at[part],
            recv_sem=c_recv.at[part],
            device_id={"scen": flip(scen, 1)},
            device_id_type=MESH,
        )

    def y_copy(index, bit, part):
        return pltpu.make_async_remote_copy(
            src_ref=mine.at[index, part],
            dst_ref=y_in.at[index, part],
            send_sem=y_send.at[index, part],
            recv_sem=y_recv.at[index, part],
            device_id={"scen": flip(scen, bit)},
            device_id_type=MESH,
        )

    for part in range(CHUNKS):
        out_half[part] = term(1 - core, part)
        c_copy(part).start()

    def t_step(index):
        t_copy(index).wait_recv()
        before = t_own[pl.ds(t_mine, t_half), :] if index == 0 else t_sum[index - 1]
        t_sum[index] = before + t_in[index]
        t_copy(index + 1).start()
        if index + 1 == len(scen_bits):
            t_all[pl.ds(t_mine, t_half), :] = t_sum[index]

    for part in range(CHUNKS):
        mine[0, part] = term(core, part)
    t_step(0)
    y_bits = scen_bits[1:]
    for part in range(CHUNKS):
        c_copy(part).wait_recv()
        mine[0, part] += in_half[part]
        y_copy(0, y_bits[0], part).start()
    for index in range(1, len(scen_bits)):
        t_step(index)
    t_copy(len(scen_bits)).wait_recv()
    whole = t_all[...]
    symmetric = 0.5 * (whole + whole.T)
    panels = window // PANEL
    inverses, lowers = [], []

    def matmul_t(lhs, rhs):
        return lax.dot_general(
            lhs, rhs, (((1,), (1,)), ((), ())),
            precision=HIGH, preferred_element_type=F32,
        )

    def next_panel(index):
        low = index * PANEL
        block = symmetric[low:, low:low + PANEL]
        for earlier in range(index):
            rest = lowers[earlier][low - earlier * PANEL:, :]
            block = block - matmul_t(rest, rest[:PANEL, :])
        inverse = panel_inverse(block[:PANEL, :], BLOCK)
        inverses.append(inverse)
        lowers.append(matmul_t(block, inverse))

    next_panel(0)

    def g_copy(part):
        start = pl.multiple_of(core * half + part * chunk, 8)
        return pltpu.make_async_remote_copy(
            src_ref=mine.at[len(y_bits), part],
            dst_ref=h_ref.at[pl.ds(start, chunk), :],
            send_sem=g_send.at[part],
            recv_sem=g_recv.at[part],
            device_id={"scen": flip(scen, 1)},
            device_id_type=MESH,
        )

    def y_step(index, part):
        y_copy(index, y_bits[index], part).wait_recv()
        total_part = mine[index, part] + y_in[index, part]
        start = pl.multiple_of(core * half + part * chunk, 8)
        if index + 1 == len(y_bits):
            total_part = total_part + (
                base[pl.ds(start, chunk), :]
                + onehot[pl.ds(start, chunk), :].astype(F32) * bsel
            )
        mine[index + 1, part] = total_part
        if index + 1 < len(y_bits):
            y_copy(index + 1, y_bits[index + 1], part).start()
        else:
            h_ref[pl.ds(start, chunk), :] = total_part
            g_copy(part).start()

    steps = [(index, part) for index in range(len(y_bits)) for part in range(CHUNKS)]
    early = len(steps) // 2
    for index, part in steps[:early]:
        y_step(index, part)
    for index in range(1, panels):
        next_panel(index)
    for index, part in steps[early:]:
        y_step(index, part)

    m_ref[...] = jnp.zeros_like(m_ref)
    for index in range(panels):
        low = index * PANEL
        for earlier in range(index):
            total = None
            for middle in range(earlier, index):
                across = lowers[middle][low - middle * PANEL:, :][:PANEL, :]
                part = jnp.dot(
                    across,
                    m_ref[middle * PANEL:(middle + 1) * PANEL,
                          earlier * PANEL:(earlier + 1) * PANEL],
                    precision=HIGH, preferred_element_type=F32,
                )
                total = part if total is None else total + part
            m_ref[low:low + PANEL, earlier * PANEL:(earlier + 1) * PANEL] = -jnp.dot(
                inverses[index], total, precision=HIGH, preferred_element_type=F32
            )
        m_ref[low:low + PANEL, low:low + PANEL] = inverses[index]
    for part in range(CHUNKS):
        g_copy(part).wait()

    for one in sent:
        one.wait_send()
    for step in range(1, n_row):
        dst = (row + step) % n_row
        rs_copy(picked.at[dst], parts.at[row], rs_send, rs_recv, dst, dst, row).wait_send()
        rs_copy(fpick.at[dst], fparts.at[row], fs_send, fs_recv, dst, dst, row).wait_send()
    for index in range(len(scen_bits) + 1):
        t_copy(index).wait_send()
    for part in range(CHUNKS):
        c_copy(part).wait_send()
        for index, bit in enumerate(y_bits):
            y_copy(index, bit, part).wait_send()


def per_device(
    n_scen, n_row,
    borders, kkt_inverse, first_section, barrier, panel_vars, probability, assignment,
):
    rows, window = first_section.shape
    depth = kkt_inverse.shape[1]
    full = kkt_inverse.shape[2]
    groups = max(1, min(n_scen, window // (8 * n_row)))
    frow = window // groups // n_row
    stages = n_scen.bit_length() - 1
    half_chunk = rows // 2 // CHUNKS
    dma = pltpu.SemaphoreType.DMA
    vmem = pl.BlockSpec(memory_space=pltpu.VMEM)
    schur, inverse = pl.pallas_call(
        functools.partial(schur_kernel, n_scen, n_row),
        out_shape=(
            jax.ShapeDtypeStruct((rows, window), F32),
            jax.ShapeDtypeStruct((window, window), F32),
        ),
        in_specs=[vmem] * 7,
        out_specs=(vmem, vmem),
        scratch_shapes=[
            pltpu.VMEM((window, SUB), jnp.int32),
            pltpu.VMEM((rows, window), BF16),
            pltpu.VMEM((n_row, depth, window), BF16),
            pltpu.VMEM((n_row, depth, window), BF16),
            pltpu.VMEM((n_row, depth, window), BF16),
            pltpu.VMEM((n_row, depth, window), BF16),
            pltpu.VMEM((n_row, frow, window), F32),
            pltpu.VMEM((n_row, frow, window), F32),
            pltpu.VMEM((n_row, frow, window), F32),
            pltpu.VMEM((rows, full), BF16),
            pltpu.VMEM((window, window), F32),
            pltpu.VMEM((stages, window // 2, window), F32),
            pltpu.VMEM((stages, window // 2, window), F32),
            pltpu.VMEM((window, window), F32),
            pltpu.VMEM((CHUNKS, half_chunk, window), F32),
            pltpu.VMEM((CHUNKS, half_chunk, window), F32),
            pltpu.VMEM((stages, CHUNKS, half_chunk, window), F32),
            pltpu.VMEM((stages - 1, CHUNKS, half_chunk, window), F32),
            *[dma((n_row,))] * 10,
            dma((stages + 1,)), dma((stages + 1,)),
            dma((CHUNKS,)), dma((CHUNKS,)),
            dma((stages - 1, CHUNKS)), dma((stages - 1, CHUNKS)),
            dma((CHUNKS,)), dma((CHUNKS,)),
        ],
        compiler_params=pltpu.CompilerParams(collective_id=0, has_side_effects=True),
    )(
        panel_vars[None, :], probability[None, :], assignment[:, None],
        barrier, borders[0], kkt_inverse[0], first_section,
    )
    return lax.dot_general(
        schur, inverse, (((1,), (1,)), ((), ())),
        precision=HIGH, preferred_element_type=F32,
    )


def solution(mesh):
    placed = (
        P("scen", None, "row"),
        P("scen", "row", None),
        P("row", None),
        P("row"),
        P(),
        P(),
        P("scen"),
    )
    return jax.shard_map(
        functools.partial(per_device, mesh.shape["scen"], mesh.shape["row"]),
        mesh=mesh, in_specs=placed, out_specs=P("row", None), check_vma=False,
    )
```

```python
import functools

import jax
import jax.numpy as jnp
from jax import lax
from jax.experimental import pallas as pl
from jax.experimental.pallas import tpu as pltpu
from jax.sharding import PartitionSpec as P

PANEL = 128
MESH = pl.DeviceIdType.MESH
HIGH = lax.Precision.HIGHEST
F32 = jnp.float32
BF16 = jnp.bfloat16
CHUNKS = 4
SUB = 8
BLOCK = 32


def small_factor(tile, first):
    shape = tile.shape
    spread = [
        jnp.broadcast_to(tile[:, first + k:first + k + 1], shape) for k in range(SUB)
    ]
    cell = {
        (i, k): jnp.broadcast_to(spread[k][i:i + 1, :], shape)
        for k in range(SUB) for i in range(k, SUB)
    }
    scale, lower = [], {}
    for j in range(SUB):
        scale.append(lax.rsqrt(cell[j, j]))
        for i in range(j + 1, SUB):
            lower[i, j] = cell[i, j] * scale[j]
        for k in range(j + 1, SUB):
            for i in range(k, SUB):
                cell[i, k] = cell[i, k] - lower[i, j] * lower[k, j]
    inverse = {}
    for j in range(SUB):
        inverse[j, j] = scale[j]
        for i in range(j + 1, SUB):
            total = lower[i, j] * inverse[j, j]
            for m in range(j + 1, i):
                total = total + lower[i, m] * inverse[m, j]
            inverse[i, j] = -(scale[i] * total)
    return inverse


def panel_inverse(block, size):
    panel = block.shape[0]
    shape = (SUB, panel)
    sub = lax.broadcasted_iota(jnp.int32, shape, 0)
    lane = lax.broadcasted_iota(jnp.int32, shape, 1)
    tiles = panel // SUB
    left = [block[low:low + SUB, :] for low in range(0, panel, SUB)]
    right = [jnp.where(lane == sub + low, 1.0, 0.0) for low in range(0, panel, SUB)]
    per = size // SUB
    for base in range(0, tiles, per):
        for own in range(base, base + per):
            first = own * SUB
            inverse = small_factor(left[own], first)
            new_left = new_right = None
            for k in range(SUB):
                coeff = inverse[SUB - 1, k]
                for i in range(SUB - 2, k - 1, -1):
                    coeff = jnp.where(sub <= i, inverse[i, k], coeff)
                if k:
                    coeff = jnp.where(sub < k, 0.0, coeff)
                add_left = coeff * left[own][k:k + 1, :]
                add_right = coeff * right[own][k:k + 1, :]
                new_left = add_left if k == 0 else new_left + add_left
                new_right = add_right if k == 0 else new_right + add_right
            for tile in range(own + 1, base + per):
                spread = [
                    jnp.broadcast_to(left[tile][:, first + m:first + m + 1], shape)
                    for m in range(SUB)
                ]
                for k in range(SUB):
                    factor = spread[0] * inverse[k, 0]
                    for m in range(1, k + 1):
                        factor = factor + spread[m] * inverse[k, m]
                    left[tile] = left[tile] - factor * new_left[k:k + 1, :]
                    right[tile] = right[tile] - factor * new_right[k:k + 1, :]
            left[own], right[own] = new_left, new_right
        if base + per < tiles:
            upper = jnp.concatenate(left[base:base + per], axis=0)
            both = jnp.concatenate(
                [upper, jnp.concatenate(right[base:base + per], axis=0)], axis=1
            )
            change = lax.dot_general(
                upper, both, (((0,), (0,)), ((), ())),
                precision=HIGH, preferred_element_type=F32,
            )
            for tile in range(base + per, tiles):
                low = tile * SUB
                left[tile] = left[tile] - change[low:low + SUB, :panel]
                right[tile] = right[tile] - change[low:low + SUB, panel:]
    return jnp.concatenate(right, axis=0)


def flip(index, bit):
    return index + bit * (1 - 2 * ((index // bit) % 2))


def toggle(index, mask):
    bit = 1
    while bit <= mask:
        if mask & bit:
            index = flip(index, bit)
        bit *= 2
    return index


def bits_down(count):
    bits = []
    bit = count // 2
    while bit >= 1:
        bits.append(bit)
        bit //= 2
    return bits


def low_bit(mask):
    return mask & -mask


def gather_blocks(arrays, me, count):
    bits = bits_down(count)

    def copy(array, owner, mask, bit):
        held, send_sem, recv_sem = array
        return pltpu.make_async_remote_copy(
            src_ref=held.at[owner],
            dst_ref=held.at[owner],
            send_sem=send_sem.at[mask],
            recv_sem=recv_sem.at[mask],
            device_id={"row": flip(me, bit)},
            device_id_type=MESH,
        )

    order = [0]
    for bit in bits:
        order += [mask + bit for mask in list(order)]
    sent = []
    for mask in order:
        for array in arrays:
            owner = toggle(me, mask)
            if mask:
                copy(array, owner, mask, low_bit(mask)).wait_recv()
            for bit in bits:
                if mask == 0 or bit < low_bit(mask):
                    one = copy(array, owner, mask + bit, bit)
                    one.start()
                    sent.append(one)
    return sent


def schur_kernel(
    n_scen, n_row,
    pv_row, prob, asg, bar_row, b_hbm, k_hbm, base_hbm,
    h_ref, m_ref,
    b_ref, k_ref, base, load_sem, rest_sem, pv_col, onehot, picked, parts, columns, solved, fpick, fparts, fall, bt,
    t_own, t_in, t_sum, t_all, out_half, in_half, mine, y_in,
    rs_send, rs_recv, fs_send, fs_recv, agc_send, agc_recv, agf_send, agf_recv,
    ags_send, ags_recv, t_send, t_recv, c_send, c_recv, y_send, y_recv,
    g_send, g_recv,
):
    scen = lax.axis_index("scen")
    row = lax.axis_index("row")
    depth = picked.shape[1]
    rows, window = base.shape
    barrier = pltpu.get_barrier_semaphore()

    def load(block):
        start = pl.multiple_of(block * depth, depth)
        return pltpu.make_async_copy(
            b_hbm.at[pl.ds(start, depth), :],
            b_ref.at[pl.ds(start, depth), :],
            load_sem.at[block],
        )

    base_load = pltpu.make_async_copy(base_hbm, base, rest_sem.at[0])
    k_load = pltpu.make_async_copy(k_hbm, k_ref, rest_sem.at[1])
    scen_bits = bits_down(n_scen)[::-1]
    for step in range(1, n_row):
        pl.semaphore_signal(
            barrier, inc=1, device_id={"row": (row + step) % n_row}, device_id_type=MESH
        )
    for bit in scen_bits:
        pl.semaphore_signal(
            barrier, inc=1, device_id={"scen": flip(scen, bit)}, device_id_type=MESH
        )

    for step in range(1, n_row + 1):
        load((row + step) % n_row).start()
    base_load.start()
    k_load.start()

    first = row * rows
    local = pv_row[...] - first
    onehot[...] = jnp.where(
        lax.broadcasted_iota(jnp.int32, (rows, window), 0) == local, 1.0, 0.0
    ).astype(BF16)

    frows = fpick.shape[0] * fpick.shape[1]
    groups = window // frows
    fstart = pl.multiple_of((scen % groups) * frows, 8)
    pv_col[...] = jnp.broadcast_to(pv_row[...], (SUB, window)).T
    flocal = pv_col[pl.ds(fstart, frows), 0:1] - first
    fhot = jnp.where(
        lax.broadcasted_iota(jnp.int32, (frows, rows), 1) == flocal, 1.0, 0.0
    ).astype(F32)

    pl.semaphore_wait(barrier, n_row - 1 + len(scen_bits))

    def pick(dst):
        load(dst).wait()
        start = pl.multiple_of(dst * depth, depth)
        block = jnp.dot(
            b_ref[pl.ds(start, depth), :], onehot[...], preferred_element_type=F32
        )
        return block.astype(BF16)

    def rs_copy(src, dst_ref, send, recv, dst, slot_send, slot_recv):
        return pltpu.make_async_remote_copy(
            src_ref=src,
            dst_ref=dst_ref,
            send_sem=send.at[slot_send],
            recv_sem=recv.at[slot_recv],
            device_id={"row": dst},
            device_id_type=MESH,
        )

    def send_pick(step, carry):
        dst = (row + step) % n_row
        picked[dst] = pick(dst)
        rs_copy(picked.at[dst], parts.at[row], rs_send, rs_recv, dst, dst, row).start()
        return carry

    lax.fori_loop(1, n_row, send_pick, 0)
    parts[row] = pick(row)

    bsel = jnp.dot(
        jnp.broadcast_to(bar_row[...].reshape(1, rows), (SUB, rows)), onehot[...].astype(F32),
        preferred_element_type=F32, precision=HIGH,
    )[0:1, :]
    slot_row = lax.broadcasted_iota(jnp.int32, (frows, window), 0) + fstart
    slot_col = lax.broadcasted_iota(jnp.int32, (frows, window), 1)
    base_load.wait()
    fpick[...] = (
        jnp.dot(fhot, base[...], preferred_element_type=F32, precision=HIGH)
        + jnp.where(slot_row == slot_col, bsel, 0.0)
    ).reshape(fpick.shape)
    for step in range(1, n_row):
        dst = (row + step) % n_row
        rs_copy(fpick.at[dst], fparts.at[row], fs_send, fs_recv, dst, dst, row).start()
    fparts[row] = fpick[row]

    def turn(tile, carry):
        start = pl.multiple_of(tile * PANEL, PANEL)
        bt[pl.ds(start, PANEL), :] = b_ref[:, pl.ds(start, PANEL)].T
        return carry

    lax.fori_loop(0, rows // PANEL, turn, 0)

    for step in range(1, n_row):
        src = (row + n_row - step) % n_row
        rs_copy(picked.at[src], parts.at[src], rs_send, rs_recv, src, src, src).wait_recv()
    total = parts[0].astype(F32)
    for slot in range(1, n_row):
        total = total + parts[slot].astype(F32)
    columns[row] = total.astype(BF16)
    for step in range(1, n_row):
        src = (row + n_row - step) % n_row
        rs_copy(fpick.at[src], fparts.at[src], fs_send, fs_recv, src, src, src).wait_recv()
    ftotal = fparts[0]
    for slot in range(1, n_row):
        ftotal = ftotal + fparts[slot]
    fall[row] = ftotal
    sent = gather_blocks(
        [(columns, agc_send, agc_recv), (fall, agf_send, agf_recv)], row, n_row
    )

    k_load.wait()
    own = jnp.dot(
        k_ref[...],
        columns[...].reshape(n_row * depth, window),
        preferred_element_type=F32,
    )
    solved[row] = own.astype(BF16)
    sent += gather_blocks([(solved, ags_send, ags_recv)], row, n_row)


    match = lax.broadcasted_iota(jnp.int32, prob.shape, 1) == asg[...]
    weight = jnp.sum(jnp.where(match, prob[...], 0.0), axis=1, keepdims=True)

    t_own[...] = weight * lax.dot_general(
        columns[...].reshape(n_row * depth, window),
        solved[...].reshape(n_row * depth, window),
        (((0,), (0,)), ((), ())),
        preferred_element_type=F32,
    )
    keep = jnp.where(scen < groups, 1.0, 0.0)
    t_own[pl.ds(fstart, frows), :] += fall[...].reshape(frows, window) * keep

    core = scen % 2
    t_half = window // 2
    t_mine = pl.multiple_of(core * t_half, 8)
    t_other = pl.multiple_of((1 - core) * t_half, 8)

    def t_copy(index):
        if index == 0:
            src, dst = t_own.at[pl.ds(t_other, t_half), :], t_in.at[0]
        elif index < len(scen_bits):
            src, dst = t_sum.at[index - 1], t_in.at[index]
        else:
            src = t_sum.at[index - 1]
            dst = t_all.at[pl.ds(t_mine, t_half), :]
        return pltpu.make_async_remote_copy(
            src_ref=src,
            dst_ref=dst,
            send_sem=t_send.at[index],
            recv_sem=t_recv.at[index],
            device_id={"scen": flip(scen, (scen_bits + [1])[index])},
            device_id_type=MESH,
        )

    t_copy(0).start()

    half = rows // 2
    chunk = half // CHUNKS
    def term(which, part):
        start = pl.multiple_of(which * half + part * chunk, 8)
        return weight * jnp.dot(
            bt[pl.ds(start, chunk), :],
            solved[...].reshape(n_row * depth, window),
            preferred_element_type=F32,
        )

    def c_copy(part):
        return pltpu.make_async_remote_copy(
            src_ref=out_half.at[part],
            dst_ref=in_half.at[part],
            send_sem=c_send.at[part],
            recv_sem=c_recv.at[part],
            device_id={"scen": flip(scen, 1)},
            device_id_type=MESH,
        )

    def y_copy(index, bit, part):
        return pltpu.make_async_remote_copy(
            src_ref=mine.at[index, part],
            dst_ref=y_in.at[index, part],
            send_sem=y_send.at[index, part],
            recv_sem=y_recv.at[index, part],
            device_id={"scen": flip(scen, bit)},
            device_id_type=MESH,
        )

    for part in range(CHUNKS):
        out_half[part] = term(1 - core, part)
        c_copy(part).start()

    def t_step(index):
        t_copy(index).wait_recv()
        before = t_own[pl.ds(t_mine, t_half), :] if index == 0 else t_sum[index - 1]
        t_sum[index] = before + t_in[index]
        t_copy(index + 1).start()
        if index + 1 == len(scen_bits):
            t_all[pl.ds(t_mine, t_half), :] = t_sum[index]

    t_step(0)
    for part in range(CHUNKS):
        mine[0, part] = term(core, part)
    y_bits = scen_bits[1:]
    for part in range(CHUNKS):
        c_copy(part).wait_recv()
        mine[0, part] += in_half[part]
        y_copy(0, y_bits[0], part).start()
    for index in range(1, len(scen_bits)):
        t_step(index)
    t_copy(len(scen_bits)).wait_recv()
    whole = t_all[...]
    symmetric = 0.5 * (whole + whole.T)
    panels = window // PANEL
    inverses, lowers = [], []

    def matmul_t(lhs, rhs):
        return lax.dot_general(
            lhs, rhs, (((1,), (1,)), ((), ())),
            precision=HIGH, preferred_element_type=F32,
        )

    def next_panel(index):
        low = index * PANEL
        block = symmetric[low:, low:low + PANEL]
        for earlier in range(index):
            rest = lowers[earlier][low - earlier * PANEL:, :]
            block = block - matmul_t(rest, rest[:PANEL, :])
        inverse = panel_inverse(block[:PANEL, :], BLOCK)
        inverses.append(inverse)
        lowers.append(matmul_t(block, inverse))

    next_panel(0)

    def g_copy(part):
        start = pl.multiple_of(core * half + part * chunk, 8)
        return pltpu.make_async_remote_copy(
            src_ref=mine.at[len(y_bits), part],
            dst_ref=h_ref.at[pl.ds(start, chunk), :],
            send_sem=g_send.at[part],
            recv_sem=g_recv.at[part],
            device_id={"scen": flip(scen, 1)},
            device_id_type=MESH,
        )

    def y_step(index, part):
        y_copy(index, y_bits[index], part).wait_recv()
        total_part = mine[index, part] + y_in[index, part]
        start = pl.multiple_of(core * half + part * chunk, 8)
        if index + 1 == len(y_bits):
            total_part = total_part + (
                base[pl.ds(start, chunk), :]
                + onehot[pl.ds(start, chunk), :].astype(F32) * bsel
            )
        mine[index + 1, part] = total_part
        if index + 1 < len(y_bits):
            y_copy(index + 1, y_bits[index + 1], part).start()
        else:
            h_ref[pl.ds(start, chunk), :] = total_part
            g_copy(part).start()

    steps = [(index, part) for index in range(len(y_bits)) for part in range(CHUNKS)]
    early = len(steps) // 2
    for index, part in steps[:early]:
        y_step(index, part)
    for index in range(1, panels):
        next_panel(index)
    for index, part in steps[early:]:
        y_step(index, part)

    m_ref[...] = jnp.zeros_like(m_ref)
    for index in range(panels):
        low = index * PANEL
        for earlier in range(index):
            total = None
            for middle in range(earlier, index):
                across = lowers[middle][low - middle * PANEL:, :][:PANEL, :]
                part = jnp.dot(
                    across,
                    m_ref[middle * PANEL:(middle + 1) * PANEL,
                          earlier * PANEL:(earlier + 1) * PANEL],
                    precision=HIGH, preferred_element_type=F32,
                )
                total = part if total is None else total + part
            m_ref[low:low + PANEL, earlier * PANEL:(earlier + 1) * PANEL] = -jnp.dot(
                inverses[index], total, precision=HIGH, preferred_element_type=F32
            )
        m_ref[low:low + PANEL, low:low + PANEL] = inverses[index]
    for part in range(CHUNKS):
        g_copy(part).wait()

    for one in sent:
        one.wait_send()
    for step in range(1, n_row):
        dst = (row + step) % n_row
        rs_copy(picked.at[dst], parts.at[row], rs_send, rs_recv, dst, dst, row).wait_send()
        rs_copy(fpick.at[dst], fparts.at[row], fs_send, fs_recv, dst, dst, row).wait_send()
    for index in range(len(scen_bits) + 1):
        t_copy(index).wait_send()
    for part in range(CHUNKS):
        c_copy(part).wait_send()
        for index, bit in enumerate(y_bits):
            y_copy(index, bit, part).wait_send()


def per_device(
    n_scen, n_row,
    borders, kkt_inverse, first_section, barrier, panel_vars, probability, assignment,
):
    rows, window = first_section.shape
    depth = kkt_inverse.shape[1]
    full = kkt_inverse.shape[2]
    groups = max(1, min(n_scen, window // (8 * n_row)))
    frow = window // groups // n_row
    stages = n_scen.bit_length() - 1
    half_chunk = rows // 2 // CHUNKS
    dma = pltpu.SemaphoreType.DMA
    vmem = pl.BlockSpec(memory_space=pltpu.VMEM)
    schur, inverse = pl.pallas_call(
        functools.partial(schur_kernel, n_scen, n_row),
        out_shape=(
            jax.ShapeDtypeStruct((rows, window), F32),
            jax.ShapeDtypeStruct((window, window), F32),
        ),
        in_specs=[vmem] * 4 + [pl.BlockSpec(memory_space=pl.ANY)] * 3,
        out_specs=(vmem, vmem),
        scratch_shapes=[
            pltpu.VMEM((full, rows), BF16),
            pltpu.VMEM((depth, full), BF16),
            pltpu.VMEM((rows, window), F32),
            dma((n_row,)), dma((2,)),
            pltpu.VMEM((window, SUB), jnp.int32),
            pltpu.VMEM((rows, window), BF16),
            pltpu.VMEM((n_row, depth, window), BF16),
            pltpu.VMEM((n_row, depth, window), BF16),
            pltpu.VMEM((n_row, depth, window), BF16),
            pltpu.VMEM((n_row, depth, window), BF16),
            pltpu.VMEM((n_row, frow, window), F32),
            pltpu.VMEM((n_row, frow, window), F32),
            pltpu.VMEM((n_row, frow, window), F32),
            pltpu.VMEM((rows, full), BF16),
            pltpu.VMEM((window, window), F32),
            pltpu.VMEM((stages, window // 2, window), F32),
            pltpu.VMEM((stages, window // 2, window), F32),
            pltpu.VMEM((window, window), F32),
            pltpu.VMEM((CHUNKS, half_chunk, window), F32),
            pltpu.VMEM((CHUNKS, half_chunk, window), F32),
            pltpu.VMEM((stages, CHUNKS, half_chunk, window), F32),
            pltpu.VMEM((stages - 1, CHUNKS, half_chunk, window), F32),
            *[dma((n_row,))] * 10,
            dma((stages + 1,)), dma((stages + 1,)),
            dma((CHUNKS,)), dma((CHUNKS,)),
            dma((stages - 1, CHUNKS)), dma((stages - 1, CHUNKS)),
            dma((CHUNKS,)), dma((CHUNKS,)),
        ],
        compiler_params=pltpu.CompilerParams(collective_id=0, has_side_effects=True),
    )(
        panel_vars[None, :], probability[None, :], assignment[:, None],
        barrier, borders[0], kkt_inverse[0], first_section,
    )
    return lax.dot_general(
        schur, inverse, (((1,), (1,)), ((), ())),
        precision=HIGH, preferred_element_type=F32,
    )


def solution(mesh):
    placed = (
        P("scen", None, "row"),
        P("scen", "row", None),
        P("row", None),
        P("row"),
        P(),
        P(),
        P("scen"),
    )
    return jax.shard_map(
        functools.partial(per_device, mesh.shape["scen"], mesh.shape["row"]),
        mesh=mesh, in_specs=placed, out_specs=P("row", None), check_vma=False,
    )
```
